32 devices in a mesh: clips: 2 (over y), seq: 8 (over z, x), mp: 2 (over core).
Axes of the slice: x: 2, y: 2, z: 4, core: 2. Of those that a mesh axis runs over, the one named last changes fastest.
Arguments:
- queries: bfloat16 [12, 4096, 128], P('mp', ('clips', 'seq')), parts along dimension 1, may hold values from -6 to 6
- keys: bfloat16 [12, 4096, 128], P('mp', ('clips', 'seq')), parts along dimension 1, may hold values from -6 to 6
- values: bfloat16 [12, 4096, 128], P('mp', ('clips', 'seq')), parts along dimension 1, may hold values from -12 to 12
- out_grad: bfloat16 [12, 4096, 128], P('mp', ('clips', 'seq')), parts along dimension 1, may hold values from -12 to 12
- tile_lists: int32 [12, 8, 4], P('mp'), may hold values from -1 to 7, as said below
Outputs:
- attn_out: bfloat16 [12, 4096, 128], P('mp', ('clips', 'seq')), parts along dimension 1
- query_grad: bfloat16 [12, 4096, 128], P('mp', ('clips', 'seq')), parts along dimension 1
- key_grad: bfloat16 [12, 4096, 128], P('mp', ('clips', 'seq')), parts along dimension 1
- value_grad: bfloat16 [12, 4096, 128], P('mp', ('clips', 'seq')), parts along dimension 1
The draws below stay inside these ranges and needn't reach their ends.
There are 2 independent parts, one for each index of `clips`. The reference program is written for one: setup_inputs(seed, part) draws one part's arguments, and reference() takes and returns one part's arrays. A program takes and returns all parts, laid end to end along the dimension named above; an argument that names none is the same for every part. Nothing has to cross between parts.
Inputs may be any that keep to these rules, and one draw needn't show every extreme that they name: `tile_lists`: tile ids count (time + row) * 8 + column over a grid of 1 x 1 x 8 tiles. Entry 0 of the list of head h and query tile q is q itself; the further entries name distinct tiles that share a face with q inside the grid, filled entries first and -1 in empty ones. For every tile and each of its six face directions, at most 3 heads of each group of 6 consecutive heads name that neighbour.
All inputs are finite; a program needn't handle non-finite values.
Results may differ from the reference program's by a relative error of at most 0.0067.
Values may be sent and summed in bfloat16 or wider, within the bound.
A program may use at most 64 MiB of HBM per device.

```python
import jax
import jax.numpy as jnp
from jax import lax

HEADS = 12
HD = 128
TILE = 256
MAXT = 4
GX = 8
GY = 1
GT = 1
TILES = 8
TOKENS = 2048


def draw_queries(key, part):
    shape_full = (HEADS, TILES, TILE, HD)
    sample = 1.4 * jax.random.normal(jax.random.fold_in(key, 1), shape_full, jnp.float32)
    return jnp.clip(sample, -6.0, 6.0).reshape(HEADS, TILES * TILE, HD).astype(jnp.bfloat16)


def draw_keys(key, part):
    shape_full = (HEADS, TILES, TILE, HD)
    sample = 1.4 * jax.random.normal(jax.random.fold_in(key, 2), shape_full, jnp.float32)
    return jnp.clip(sample, -6.0, 6.0).reshape(HEADS, TILES * TILE, HD).astype(jnp.bfloat16)


def shuffle_six(subkey):
    return jax.random.permutation(subkey, 6)


def draw_tile_lists(key, part):
    groups = HEADS // 6
    tile_ids = jnp.arange(TILES, dtype=jnp.int32)
    across = tile_ids % GX
    downward = tile_ids // GX % GY
    frames = tile_ids // (GX * GY)
    layer_size = GX * GY
    neighbour_ids = jnp.stack([tile_ids + 1, tile_ids - 1, tile_ids + GX, tile_ids - GX, tile_ids + layer_size, tile_ids - layer_size], axis=-1)
    inside = jnp.stack([across < GX - 1, across > 0, downward < GY - 1, downward > 0, frames < GT - 1, frames > 0], axis=-1)
    row_shift = jax.vmap(shuffle_six)(jax.random.split(jax.random.fold_in(key, 5), TILES * groups)).reshape(TILES, groups, 6)
    column_shift = jax.vmap(shuffle_six)(jax.random.split(jax.random.fold_in(key, 6), TILES * groups)).reshape(TILES, groups, 6)
    latin_square = (row_shift[:, :, :, None] + column_shift[:, :, None, :]) % 6 < 3
    frame_pick = jnp.minimum(jax.random.randint(jax.random.fold_in(key, 11), (), 1, max(2, GT - 1)), GT - 1)
    row_pick = jnp.minimum(jax.random.randint(jax.random.fold_in(key, 12), (), 1, max(2, GY - 1)), GY - 1)
    column_pick = jax.random.randint(jax.random.fold_in(key, 13), (), 1, GX - 1)
    forced = (frame_pick * GY + row_pick) * GX + column_pick
    level_draw = jax.random.randint(jax.random.fold_in(key, 7), (TILES,), 1, 4)
    levels = jnp.where(tile_ids == forced, 3, level_draw)
    coin_draw = jax.random.randint(jax.random.fold_in(key, 9), (TILES, groups, 6, 6), 0, 3)
    in_use = latin_square & (coin_draw < levels[:, None, None, None]) & inside[:, None, None, :]
    ranking = jnp.cumsum(in_use.astype(jnp.int32), axis=-1)
    entries = [jnp.broadcast_to(tile_ids[:, None, None], (TILES, groups, 6))]
    for position in range(1, MAXT):
        matched = in_use & (ranking == position)
        picked = jnp.sum(jnp.where(matched, neighbour_ids[:, None, None, :], 0), axis=-1)
        entries.append(jnp.where(jnp.any(matched, axis=-1), picked, -1))
    lists_table = jnp.stack(entries, axis=-1)
    return jnp.transpose(lists_table, (1, 2, 0, 3)).reshape(HEADS, TILES, MAXT).astype(jnp.int32)


def level_of(own_key, extent, pieces, low, largest):
    gain, own = 1.0, jax.random.fold_in(own_key, 6)
    for axis_at, parts in pieces:
        draws = jnp.exp(jax.random.uniform(jax.random.fold_in(own, axis_at), (parts,), jnp.float32, low / len(pieces), largest / len(pieces)))
        gain = gain * jnp.repeat(draws, extent[axis_at] // parts).reshape([-1 if axis == axis_at else 1 for axis in range(len(extent))])
    return gain


def bell_draw(stream_key, dims, scale, reach, cuts=(), kind=jnp.bfloat16):
    result = scale * jax.random.normal(stream_key, dims, jnp.float32)
    if cuts:
        result = result * level_of(stream_key, dims, cuts, -0.22, 0.18)
    return jnp.clip(result, -reach, reach).astype(kind)


def setup_inputs(seed: int = 0, part: int = 0) -> dict:
    splits = jax.random.split(jax.random.key(seed), 6)
    own_keys = jax.random.split(jax.random.fold_in(splits[5], part), 6)
    queries = draw_queries(jax.random.fold_in(jax.random.fold_in(splits[5], part), 71), part)
    keys = draw_keys(jax.random.fold_in(jax.random.fold_in(splits[5], part), 71), part)
    values = bell_draw(own_keys[2], (HEADS, TOKENS, HD), 2.0, 12.0, ((0, 2), (1, 8)))
    out_grad = bell_draw(own_keys[3], (HEADS, TOKENS, HD), 2.0, 12.0, ((0, 2), (1, 8)))
    tile_lists = draw_tile_lists(jax.random.fold_in(splits[5], 71), part)
    return dict(queries=queries, keys=keys, values=values, out_grad=out_grad, tile_lists=tile_lists)


def head_pass(operands):
    query_tiles, key_tiles, value_tiles, grad_tiles, head_lists = operands
    score_scale = HD ** -0.5
    live_slots = head_lists >= 0
    safe_lists = jnp.where(live_slots, head_lists, 0).astype(jnp.int32)
    key_chosen = key_tiles[safe_lists].astype(jnp.float32)
    value_chosen = value_tiles[safe_lists].astype(jnp.float32)
    query_wide = query_tiles.astype(jnp.float32)
    grad_wide = grad_tiles.astype(jnp.float32)
    scores = jnp.einsum('aid,ajtd->aijt', query_wide, key_chosen) * score_scale
    scores = jnp.where(live_slots[:, None, :, None], scores, -jnp.inf)
    row_max = jnp.max(scores, axis=(2, 3), keepdims=True)
    weights = jnp.exp(scores - row_max)
    probs = weights / jnp.sum(weights, axis=(2, 3), keepdims=True)
    probs_low = lax.optimization_barrier(probs.astype(jnp.bfloat16)).astype(jnp.float32)
    attention = jnp.einsum('aijt,ajtd->aid', probs_low, value_chosen).astype(jnp.bfloat16)
    prob_grad = jnp.einsum('aid,ajtd->aijt', grad_wide, value_chosen)
    delta = jnp.sum(probs * prob_grad, axis=(2, 3), keepdims=True)
    score_grad = lax.optimization_barrier((probs * (prob_grad - delta)).astype(jnp.bfloat16)).astype(jnp.float32)
    query_result = (jnp.einsum('aijt,ajtd->aid', score_grad, key_chosen) * score_scale).astype(jnp.bfloat16)
    key_part = (jnp.einsum('aijt,aid->ajtd', score_grad, query_wide) * score_scale).astype(jnp.bfloat16)
    value_part = jnp.einsum('aijt,aid->ajtd', probs_low, grad_wide).astype(jnp.bfloat16)
    live_wide = live_slots[:, :, None, None]
    key_total = jnp.zeros((TILES, TILE, HD), jnp.float32).at[safe_lists].add(
        jnp.where(live_wide, key_part.astype(jnp.float32), 0.0))
    value_total = jnp.zeros((TILES, TILE, HD), jnp.float32).at[safe_lists].add(
        jnp.where(live_wide, value_part.astype(jnp.float32), 0.0))
    return attention, query_result, key_total.astype(jnp.bfloat16), value_total.astype(jnp.bfloat16)


def reference(queries, keys, values, out_grad, tile_lists):
    shaped = (HEADS, TILES, TILE, HD)
    operands = (queries.reshape(shaped), keys.reshape(shaped), values.reshape(shaped),
                out_grad.reshape(shaped), tile_lists.astype(jnp.int32))
    attention, query_result, key_result, value_result = lax.map(head_pass, operands)
    flat = (HEADS, TOKENS, HD)
    return (attention.reshape(flat), query_result.reshape(flat),
            key_result.reshape(flat), value_result.reshape(flat))
```

```python
import functools

import jax
import jax.numpy as jnp
from jax import lax
from jax.experimental import pallas as pl
from jax.experimental.pallas import tpu as pltpu
from jax.sharding import PartitionSpec as P

HCAP = 3
GX = 8
MASKED = -1e30


def directions(tile_count):
    row_tiles = min(4, tile_count // GX)
    layer_size = GX * row_tiles
    layers = tile_count // layer_size
    result = []
    for stride, extent in ((1, GX), (GX, row_tiles), (layer_size, layers)):
        if extent > 1:
            result += [(stride, extent, 1), (stride, extent, -1)]
    return result


def dot_rows(a, b):
    return lax.dot_general(a, b, (((1,), (1,)), ((), ())), preferred_element_type=jnp.float32)


def dot_plain(a, b):
    return lax.dot_general(a, b, (((1,), (0,)), ((), ())), preferred_element_type=jnp.float32)


def dot_first(a, b):
    return lax.dot_general(a, b, (((0,), (0,)), ((), ())), preferred_element_type=jnp.float32)


def kernel(
    dims,
    lists,
    q,
    k,
    v,
    g,
    out,
    qg,
    kg,
    vg,
    k_pack,
    v_pack,
    k_in,
    v_in,
    kp_pack,
    vp_pack,
    kp_in,
    vp_in,
    p32,
    p16,
    s16,
    kg32,
    vg32,
    read_slot,
    owed_slot,
    f_send,
    f_recv,
    b_send,
    b_recv,
):
    tile_count, entries, cap = dims
    heads, rows, width = q.shape
    scale = width ** (-0.5)
    dirs = directions(tile_count)
    nd = len(dirs)
    E = nd + 1
    none = nd * cap
    me = lax.axis_index("seq")

    inside, beside = [], []
    for stride, extent, sign in dirs:
        at = (me // stride) % extent + sign
        ok = (at >= 0) & (at < extent)
        inside.append(ok)
        beside.append(jnp.where(ok, me + sign * stride, me))

    barrier = pltpu.get_barrier_semaphore()
    for d in range(nd):

        @pl.when(inside[d])
        def _(d=d):
            pl.semaphore_signal(
                barrier,
                inc=1,
                device_id={"seq": beside[d]},
                device_id_type=pl.DeviceIdType.MESH,
            )

    def table(reader, named, ok, slot_ref, d):
        count = jnp.int32(0)
        held = [jnp.int32(0)] * cap
        for h in range(heads):
            hit = jnp.int32(0)
            for j in range(1, entries):
                entry = lists[(h * tile_count + reader) * entries + j]
                hit = hit | (entry == named).astype(jnp.int32)
            hit = hit * ok.astype(jnp.int32)
            slot_ref[d * heads + h] = jnp.where(
                hit == 1, d * cap + jnp.minimum(count, cap - 1), none
            )
            held = [
                jnp.where((hit == 1) & (count == s), jnp.int32(h), held[s]) for s in range(cap)
            ]
            count = count + hit
        return held

    owed_head = [table(beside[d], me, inside[d], owed_slot, d) for d in range(nd)]
    for d in range(nd):
        for s in range(cap):
            k_pack[d * cap + s] = k[owed_head[d][s]]
    for d in range(nd):
        for s in range(cap):
            v_pack[d * cap + s] = v[owed_head[d][s]]

    pl.semaphore_wait(barrier, sum(ok.astype(jnp.int32) for ok in inside))

    def forward(kind, d, to):
        src, dst = ((k_pack, k_in), (v_pack, v_in))[kind]
        return pltpu.make_async_remote_copy(
            src_ref=src.at[pl.ds(d * cap, cap)],
            dst_ref=dst.at[pl.ds(to * cap, cap)],
            send_sem=f_send.at[kind, d],
            recv_sem=f_recv.at[kind, to],
            device_id={"seq": beside[d]},
            device_id_type=pl.DeviceIdType.MESH,
        )

    def backward(kind, d, s, to):
        src, dst = ((vp_pack, vp_in), (kp_pack, kp_in))[kind]
        return pltpu.make_async_remote_copy(
            src_ref=src.at[d * cap + s],
            dst_ref=dst.at[to * cap + s],
            send_sem=b_send.at[kind, d * cap + s],
            recv_sem=b_recv.at[kind, to * cap + s],
            device_id={"seq": beside[d]},
            device_id_type=pl.DeviceIdType.MESH,
        )

    for kind in range(2):
        for d in range(nd):

            @pl.when(inside[d])
            def _(kind=kind, d=d):
                forward(kind, d, d ^ 1).start()

    read_head = [table(me, beside[d], inside[d], read_slot, d) for d in range(nd)]
    blank = jnp.zeros((rows, width), q.dtype)
    k_in[none] = blank
    v_in[none] = blank
    kp_in[none] = blank
    vp_in[none] = blank

    def own_scores(h, carry):
        p32[h * E] = dot_rows(k[h], q[h]) * scale
        return carry

    lax.fori_loop(0, heads, own_scores, 0)

    def arrived(kind):
        for d in range(nd):

            @pl.when(inside[d])
            def _(d=d):
                forward(kind, d, d).wait_recv()

    arrived(0)

    def softmax(h, carry):
        scores = [p32[h * E]]
        for d in range(nd):
            slot = read_slot[d * heads + h]
            bias = jnp.where(slot == none, jnp.float32(MASKED), jnp.float32(0.0))
            scores.append(dot_rows(k_in[slot], q[h]) * scale + bias)
        top = functools.reduce(
            jnp.maximum, [jnp.max(s, axis=0, keepdims=True) for s in scores]
        )
        weights = [jnp.exp(s - top) for s in scores]
        total = sum(jnp.sum(w, axis=0, keepdims=True) for w in weights)
        inverse = 1.0 / total
        for e in range(E):
            prob = weights[e] * inverse
            p32[h * E + e] = prob
            p16[h * E + e] = prob.astype(p16.dtype)
        return carry

    lax.fori_loop(0, heads, softmax, 0)

    for d in range(nd):
        for s in range(cap):
            h = read_head[d][s]
            part = dot_plain(p16[h * E + d + 1], g[h])
            vp_pack[d * cap + s] = part.astype(vp_pack.dtype)
        for s in range(cap):

            @pl.when(inside[d])
            def _(d=d, s=s):
                backward(0, d, s, d ^ 1).start()

    arrived(1)

    def score_grads(h, carry):
        blocks = [v[h]] + [v_in[read_slot[d * heads + h]] for d in range(nd)]
        grads = [dot_rows(block, g[h]) for block in blocks]
        delta = sum(
            jnp.sum(p32[h * E + e] * grads[e], axis=0, keepdims=True) for e in range(E)
        )
        for e in range(E):
            s16[h * E + e] = (p32[h * E + e] * (grads[e] - delta)).astype(s16.dtype)
        return carry

    lax.fori_loop(0, heads, score_grads, 0)

    for d in range(nd):
        for s in range(cap):
            h = read_head[d][s]
            part = dot_plain(s16[h * E + d + 1], q[h]) * scale
            kp_pack[d * cap + s] = part.astype(kp_pack.dtype)
        for s in range(cap):

            @pl.when(inside[d])
            def _(d=d, s=s):
                backward(1, d, s, d ^ 1).start()

    def own_results(h, carry):
        slots = [read_slot[d * heads + h] for d in range(nd)]
        attn = dot_first(p16[h * E], v[h])
        grad = dot_first(s16[h * E], k[h])
        for d in range(nd):
            attn += dot_first(p16[h * E + d + 1], v_in[slots[d]])
            grad += dot_first(s16[h * E + d + 1], k_in[slots[d]])
        out[h] = attn.astype(out.dtype)
        qg[h] = (grad * scale).astype(qg.dtype)
        kg32[h] = dot_plain(s16[h * E], q[h]) * scale
        vg32[h] = dot_plain(p16[h * E], g[h])
        return carry

    lax.fori_loop(0, heads, own_results, 0)

    for kind, total, terms, result in ((0, vg32, vp_in, vg), (1, kg32, kp_in, kg)):
        for d in range(nd):

            @pl.when(inside[d])
            def _(kind=kind, d=d):
                for s in range(cap):
                    backward(kind, d, s, d).wait_recv()

        def add_terms(h, carry, total=total, terms=terms, result=result):
            value = total[h]
            for d in range(nd):
                value += terms[owed_slot[d * heads + h]].astype(jnp.float32)
            result[h] = value.astype(result.dtype)
            return carry

        lax.fori_loop(0, heads, add_terms, 0)

    for kind in range(2):
        for d in range(nd):

            @pl.when(inside[d])
            def _(kind=kind, d=d):
                forward(kind, d, d ^ 1).wait_send()
                for s in range(cap):
                    backward(kind, d, s, d ^ 1).wait_send()


def per_device(queries, keys, values, out_grad, tile_lists):
    heads, rows, width = queries.shape
    tile_count = lax.axis_size("seq")
    entries = tile_lists.shape[2]
    cap = HCAP * max(1, heads // 6)
    nd = len(directions(tile_count))
    E = nd + 1
    low = queries.dtype
    shape = jax.ShapeDtypeStruct(queries.shape, low)
    vmem = pl.BlockSpec(memory_space=pltpu.VMEM)
    packed = pltpu.VMEM((nd * cap, rows, width), low)
    landed = pltpu.VMEM((nd * cap + 1, rows, width), low)
    wide = pltpu.VMEM((heads, rows, width), jnp.float32)
    return pl.pallas_call(
        functools.partial(kernel, (tile_count, entries, cap)),
        out_shape=(shape,) * 4,
        in_specs=[pl.BlockSpec(memory_space=pltpu.SMEM)] + [vmem] * 4,
        out_specs=(vmem,) * 4,
        scratch_shapes=[
            packed,
            packed,
            landed,
            landed,
            packed,
            packed,
            landed,
            landed,
            pltpu.VMEM((heads * E, rows, rows), jnp.float32),
            pltpu.VMEM((heads * E, rows, rows), low),
            pltpu.VMEM((heads * E, rows, rows), low),
            wide,
            wide,
            pltpu.SMEM((nd * heads,), jnp.int32),
            pltpu.SMEM((nd * heads,), jnp.int32),
            pltpu.SemaphoreType.DMA((2, nd)),
            pltpu.SemaphoreType.DMA((2, nd)),
            pltpu.SemaphoreType.DMA((2, nd * cap)),
            pltpu.SemaphoreType.DMA((2, nd * cap)),
        ],
        compiler_params=pltpu.CompilerParams(
            collective_id=0, has_side_effects=True, vmem_limit_bytes=60 * 1024 * 1024
        ),
        name="tile_attention",
    )(tile_lists.reshape(-1), queries, keys, values, out_grad)


def solution(mesh):
    tokens = P("mp", ("clips", "seq"), None)
    return jax.shard_map(
        per_device,
        mesh=mesh,
        in_specs=(tokens, tokens, tokens, tokens, P("mp", None, None)),
        out_specs=(tokens,) * 4,
        check_vma=False,
    )
```

```python
import functools

import jax
import jax.numpy as jnp
from jax import lax
from jax.experimental import pallas as pl
from jax.experimental.pallas import tpu as pltpu
from jax.sharding import PartitionSpec as P

HCAP = 3
GX = 8
MASKED = -1e30


def directions(tile_count):
    row_tiles = min(4, tile_count // GX)
    layer_size = GX * row_tiles
    layers = tile_count // layer_size
    result = []
    for stride, extent in ((1, GX), (GX, row_tiles), (layer_size, layers)):
        if extent > 1:
            result += [(stride, extent, 1), (stride, extent, -1)]
    return result


def dot_rows(a, b):
    return lax.dot_general(a, b, (((1,), (1,)), ((), ())), preferred_element_type=jnp.float32)


def dot_plain(a, b):
    return lax.dot_general(a, b, (((1,), (0,)), ((), ())), preferred_element_type=jnp.float32)


def dot_first(a, b):
    return lax.dot_general(a, b, (((0,), (0,)), ((), ())), preferred_element_type=jnp.float32)


def kernel(
    dims,
    lists,
    q_hbm,
    k_hbm,
    v_hbm,
    g_hbm,
    out_hbm,
    qg_hbm,
    kg_hbm,
    vg_hbm,
    q,
    k,
    v,
    g,
    out,
    qg,
    kg,
    vg,
    k_pack,
    v_pack,
    k_in,
    v_in,
    kp_pack,
    vp_pack,
    kp_in,
    vp_in,
    p32,
    p16,
    s16,
    kg32,
    vg32,
    read_slot,
    owed_slot,
    f_send,
    f_recv,
    b_send,
    b_recv,
    i_sem,
    o_sem,
):
    tile_count, entries, cap = dims
    heads, rows, width = q.shape
    scale = width ** (-0.5)
    dirs = directions(tile_count)
    nd = len(dirs)
    E = nd + 1
    none = nd * cap
    me = lax.axis_index("seq")

    loads = [
        pltpu.make_async_copy(src, dst, i_sem.at[n])
        for n, (src, dst) in enumerate(((k_hbm, k), (v_hbm, v), (q_hbm, q), (g_hbm, g)))
    ]
    for load in loads:
        load.start()
    stores = [
        pltpu.make_async_copy(src, dst, o_sem.at[n])
        for n, (src, dst) in enumerate(((out, out_hbm), (qg, qg_hbm), (vg, vg_hbm), (kg, kg_hbm)))
    ]

    inside, beside = [], []
    for stride, extent, sign in dirs:
        at = (me // stride) % extent + sign
        ok = (at >= 0) & (at < extent)
        inside.append(ok)
        beside.append(jnp.where(ok, me + sign * stride, me))

    barrier = pltpu.get_barrier_semaphore()
    for d in range(nd):

        @pl.when(inside[d])
        def _(d=d):
            pl.semaphore_signal(
                barrier,
                inc=1,
                device_id={"seq": beside[d]},
                device_id_type=pl.DeviceIdType.MESH,
            )

    def table(reader, named, ok, slot_ref, d):
        count = jnp.int32(0)
        held = [jnp.int32(0)] * cap
        for h in range(heads):
            hit = jnp.int32(0)
            for j in range(1, entries):
                entry = lists[h, j, reader]
                hit = hit | (entry == named).astype(jnp.int32)
            hit = hit * ok.astype(jnp.int32)
            slot_ref[d * heads + h] = jnp.where(
                hit == 1, d * cap + jnp.minimum(count, cap - 1), none
            )
            held = [
                jnp.where((hit == 1) & (count == s), jnp.int32(h), held[s]) for s in range(cap)
            ]
            count = count + hit
        return held

    owed_head = [table(beside[d], me, inside[d], owed_slot, d) for d in range(nd)]
    def forward(kind, d, to):
        src, dst = ((k_pack, k_in), (v_pack, v_in))[kind]
        return pltpu.make_async_remote_copy(
            src_ref=src.at[pl.ds(d * cap, cap)],
            dst_ref=dst.at[pl.ds(to * cap, cap)],
            send_sem=f_send.at[kind, d],
            recv_sem=f_recv.at[kind, to],
            device_id={"seq": beside[d]},
            device_id_type=pl.DeviceIdType.MESH,
        )

    def backward(kind, d, s, to):
        src, dst = ((vp_pack, vp_in), (kp_pack, kp_in))[kind]
        return pltpu.make_async_remote_copy(
            src_ref=src.at[d * cap + s],
            dst_ref=dst.at[to * cap + s],
            send_sem=b_send.at[kind, d * cap + s],
            recv_sem=b_recv.at[kind, to * cap + s],
            device_id={"seq": beside[d]},
            device_id_type=pl.DeviceIdType.MESH,
        )

    for kind, (full, pack) in enumerate(((k, k_pack), (v, v_pack))):
        loads[kind].wait()
        for d in range(nd):
            for s in range(cap):
                pack[d * cap + s] = full[owed_head[d][s]]
        if kind == 0:
            pl.semaphore_wait(barrier, sum(ok.astype(jnp.int32) for ok in inside))
        for d in range(nd):

            @pl.when(inside[d])
            def _(kind=kind, d=d):
                forward(kind, d, d ^ 1).start()

    read_head = [table(me, beside[d], inside[d], read_slot, d) for d in range(nd)]
    blank = jnp.zeros((rows, width), q.dtype)
    k_in[none] = blank
    v_in[none] = blank
    kp_in[none] = blank
    vp_in[none] = blank
    loads[2].wait()
    loads[3].wait()

    def own_scores(h, carry):
        p32[h * E] = dot_rows(k[h], q[h]) * scale
        return carry

    lax.fori_loop(0, heads, own_scores, 0)

    def arrived(kind):
        for d in range(nd):

            @pl.when(inside[d])
            def _(d=d):
                forward(kind, d, d).wait_recv()

    arrived(0)

    def softmax(h, carry):
        scores = [p32[h * E]]
        for d in range(nd):
            slot = read_slot[d * heads + h]
            bias = jnp.where(slot == none, jnp.float32(MASKED), jnp.float32(0.0))
            scores.append(dot_rows(k_in[slot], q[h]) * scale + bias)
        top = functools.reduce(
            jnp.maximum, [jnp.max(s, axis=0, keepdims=True) for s in scores]
        )
        weights = [jnp.exp(s - top) for s in scores]
        total = sum(jnp.sum(w, axis=0, keepdims=True) for w in weights)
        inverse = 1.0 / total
        for e in range(E):
            prob = weights[e] * inverse
            p32[h * E + e] = prob
            p16[h * E + e] = prob.astype(p16.dtype)
        return carry

    lax.fori_loop(0, heads, softmax, 0)

    for d in range(nd):
        for s in range(cap):
            h = read_head[d][s]
            part = dot_plain(p16[h * E + d + 1], g[h])
            vp_pack[d * cap + s] = part.astype(vp_pack.dtype)
        for s in range(cap):

            @pl.when(inside[d])
            def _(d=d, s=s):
                backward(0, d, s, d ^ 1).start()

    arrived(1)

    def score_grads(h, carry):
        blocks = [v[h]] + [v_in[read_slot[d * heads + h]] for d in range(nd)]
        grads = [dot_rows(block, g[h]) for block in blocks]
        delta = sum(
            jnp.sum(p32[h * E + e] * grads[e], axis=0, keepdims=True) for e in range(E)
        )
        for e in range(E):
            s16[h * E + e] = (p32[h * E + e] * (grads[e] - delta)).astype(s16.dtype)
        return carry

    lax.fori_loop(0, heads, score_grads, 0)

    for d in range(nd):
        for s in range(cap):
            h = read_head[d][s]
            part = dot_plain(s16[h * E + d + 1], q[h]) * scale
            kp_pack[d * cap + s] = part.astype(kp_pack.dtype)
        for s in range(cap):

            @pl.when(inside[d])
            def _(d=d, s=s):
                backward(1, d, s, d ^ 1).start()

    def own_results(h, carry):
        slots = [read_slot[d * heads + h] for d in range(nd)]
        attn = dot_first(p16[h * E], v[h])
        grad = dot_first(s16[h * E], k[h])
        for d in range(nd):
            attn += dot_first(p16[h * E + d + 1], v_in[slots[d]])
            grad += dot_first(s16[h * E + d + 1], k_in[slots[d]])
        out[h] = attn.astype(out.dtype)
        qg[h] = (grad * scale).astype(qg.dtype)
        kg32[h] = dot_plain(s16[h * E], q[h]) * scale
        vg32[h] = dot_plain(p16[h * E], g[h])
        return carry

    lax.fori_loop(0, heads, own_results, 0)
    stores[0].start()
    stores[1].start()

    for kind, total, terms, result in ((0, vg32, vp_in, vg), (1, kg32, kp_in, kg)):
        for d in range(nd):

            @pl.when(inside[d])
            def _(kind=kind, d=d):
                for s in range(cap):
                    backward(kind, d, s, d).wait_recv()

        def add_terms(h, carry, total=total, terms=terms, result=result):
            value = total[h]
            for d in range(nd):
                value += terms[owed_slot[d * heads + h]].astype(jnp.float32)
            result[h] = value.astype(result.dtype)
            return carry

        lax.fori_loop(0, heads, add_terms, 0)
        stores[2 + kind].start()

    for kind in range(2):
        for d in range(nd):

            @pl.when(inside[d])
            def _(kind=kind, d=d):
                forward(kind, d, d ^ 1).wait_send()
                for s in range(cap):
                    backward(kind, d, s, d ^ 1).wait_send()
    for store in stores:
        store.wait()


def write_results(*refs):
    count = (len(refs) - 2) // 3
    sources, results, held = refs[:count], refs[count : 2 * count], refs[2 * count : 3 * count]
    in_sem, out_sem = refs[3 * count :]
    loads = [pltpu.make_async_copy(a, b, in_sem.at[n]) for n, (a, b) in enumerate(zip(sources, held))]
    stores = [pltpu.make_async_copy(a, b, out_sem.at[n]) for n, (a, b) in enumerate(zip(held, results))]
    for load in loads:
        load.start()
    for load, store in zip(loads, stores):
        load.wait()
        store.start()
    for store in stores:
        store.wait()


def per_device(queries, keys, values, out_grad, tile_lists):
    heads, rows, width = queries.shape
    tile_count = lax.axis_size("seq")
    entries = tile_lists.shape[2]
    cap = HCAP * max(1, heads // 6)
    nd = len(directions(tile_count))
    E = nd + 1
    low = queries.dtype
    shape = jax.ShapeDtypeStruct(queries.shape, low)
    anywhere = pl.BlockSpec(memory_space=pl.ANY)
    whole = pltpu.VMEM(queries.shape, low)
    packed = pltpu.VMEM((nd * cap, rows, width), low)
    landed = pltpu.VMEM((nd * cap + 1, rows, width), low)
    wide = pltpu.VMEM((heads, rows, width), jnp.float32)
    results = pl.pallas_call(
        functools.partial(kernel, (tile_count, entries, cap)),
        out_shape=(shape,) * 4,
        in_specs=[pl.BlockSpec(memory_space=pltpu.SMEM)] + [anywhere] * 4,
        out_specs=(anywhere,) * 4,
        scratch_shapes=[whole] * 8
        + [
            packed,
            packed,
            landed,
            landed,
            packed,
            packed,
            landed,
            landed,
            pltpu.VMEM((heads * E, rows, rows), jnp.float32),
            pltpu.VMEM((heads * E, rows, rows), low),
            pltpu.VMEM((heads * E, rows, rows), low),
            wide,
            wide,
            pltpu.SMEM((nd * heads,), jnp.int32),
            pltpu.SMEM((nd * heads,), jnp.int32),
            pltpu.SemaphoreType.DMA((2, nd)),
            pltpu.SemaphoreType.DMA((2, nd)),
            pltpu.SemaphoreType.DMA((2, nd * cap)),
            pltpu.SemaphoreType.DMA((2, nd * cap)),
            pltpu.SemaphoreType.DMA((4,)),
            pltpu.SemaphoreType.DMA((4,)),
        ],
        compiler_params=pltpu.CompilerParams(
            collective_id=0, has_side_effects=True, vmem_limit_bytes=60 * 1024 * 1024
        ),
        name="tile_attention",
    )(jnp.swapaxes(tile_lists, 1, 2), queries, keys, values, out_grad)
    return pl.pallas_call(
        write_results,
        out_shape=(shape,) * 4,
        in_specs=[anywhere] * 4,
        out_specs=(anywhere,) * 4,
        scratch_shapes=[whole] * 4
        + [pltpu.SemaphoreType.DMA((4,)), pltpu.SemaphoreType.DMA((4,))],
        compiler_params=pltpu.CompilerParams(vmem_limit_bytes=60 * 1024 * 1024),
        name="write_results",
    )(*results)


def solution(mesh):
    tokens = P("mp", ("clips", "seq"), None)
    return jax.shard_map(
        per_device,
        mesh=mesh,
        in_specs=(tokens, tokens, tokens, tokens, P("mp", None, None)),
        out_specs=(tokens,) * 4,
        check_vma=False,
    )
```

```python
import functools

import jax
import jax.numpy as jnp
from jax import lax
from jax.experimental import pallas as pl
from jax.experimental.pallas import tpu as pltpu
from jax.sharding import PartitionSpec as P

HCAP = 3
GX = 8
MASKED = -1e30


def directions(tile_count):
    row_tiles = min(4, tile_count // GX)
    layer_size = GX * row_tiles
    layers = tile_count // layer_size
    result = []
    for stride, extent in ((1, GX), (GX, row_tiles), (layer_size, layers)):
        if extent > 1:
            result += [(stride, extent, 1), (stride, extent, -1)]
    return result


def dot_rows(a, b):
    return lax.dot_general(a, b, (((1,), (1,)), ((), ())), preferred_element_type=jnp.float32)


def dot_plain(a, b):
    return lax.dot_general(a, b, (((1,), (0,)), ((), ())), preferred_element_type=jnp.float32)


def dot_first(a, b):
    return lax.dot_general(a, b, (((0,), (0,)), ((), ())), preferred_element_type=jnp.float32)


def kernel(
    dims,
    lists,
    q_hbm,
    k_hbm,
    v_hbm,
    g_hbm,
    out_hbm,
    qg_hbm,
    kg_hbm,
    vg_hbm,
    q,
    k,
    v,
    g,
    out,
    qg,
    kg,
    vg,
    k_pack,
    v_pack,
    k_in,
    v_in,
    kp_pack,
    vp_pack,
    kp_in,
    vp_in,
    p32,
    p16,
    s16,
    kg32,
    vg32,
    read_slot,
    owed_slot,
    relay_in,
    send_sem,
    recv_sem,
    relay_send,
    relay_recv,
    i_sem,
    o_sem,
):
    tile_count, entries, cap, chunks = dims
    heads, rows, width = q.shape
    scale = width ** (-0.5)
    dirs = directions(tile_count)
    nd = len(dirs)
    E = nd + 1
    none = nd * cap
    me = lax.axis_index("seq")

    loads = [
        pltpu.make_async_copy(src, dst, i_sem.at[n])
        for n, (src, dst) in enumerate(((k_hbm, k), (v_hbm, v), (q_hbm, q), (g_hbm, g)))
    ]
    for load in loads:
        load.start()
    stores = [
        pltpu.make_async_copy(src, dst, o_sem.at[n])
        for n, (src, dst) in enumerate(((out, out_hbm), (qg, qg_hbm), (vg, vg_hbm), (kg, kg_hbm)))
    ]

    inside, beside = [], []
    for stride, extent, sign in dirs:
        at = (me // stride) % extent + sign
        ok = (at >= 0) & (at < extent)
        inside.append(ok)
        beside.append(jnp.where(ok, me + sign * stride, me))

    chunk_rows = rows // chunks
    even, place = me % 2 == 0, me // 2
    by_relay = [[False] * chunks for _ in range(nd)]
    hands_on = [[False] * chunks for _ in range(nd)]
    two_on = []
    greeted = [(inside[d], beside[d]) for d in range(nd)]
    if chunks > 1:
        for d, (_, _, sign) in enumerate(dirs):
            amount = chunks - 1 - place if sign > 0 else place
            sends = jnp.logical_not(even) if sign > 0 else even
            by_relay[d] = [sends & (c < amount) for c in range(chunks)]
            hands_on[d] = [jnp.logical_not(sends) & (c < amount) for c in range(chunks)]
            ok = (me + 2 * sign >= 0) & (me + 2 * sign < tile_count)
            two_on.append(jnp.where(ok, me + 2 * sign, me))
            greeted.append((ok, two_on[d]))

    barrier = pltpu.get_barrier_semaphore()
    for ok, other in greeted:

        @pl.when(ok)
        def _(other=other):
            pl.semaphore_signal(
                barrier,
                inc=1,
                device_id={"seq": other},
                device_id_type=pl.DeviceIdType.MESH,
            )

    def table(reader, named, ok, slot_ref, d):
        count = jnp.int32(0)
        held = [jnp.int32(0)] * cap
        for h in range(heads):
            hit = jnp.int32(0)
            for j in range(1, entries):
                entry = lists[h, j, reader]
                hit = hit | (entry == named).astype(jnp.int32)
            hit = hit * ok.astype(jnp.int32)
            slot_ref[d * heads + h] = jnp.where(
                hit == 1, d * cap + jnp.minimum(count, cap - 1), none
            )
            held = [
                jnp.where((hit == 1) & (count == s), jnp.int32(h), held[s]) for s in range(cap)
            ]
            count = count + hit
        return held

    owed_head = [table(beside[d], me, inside[d], owed_slot, d) for d in range(nd)]
    packs = (k_pack, v_pack, vp_pack, kp_pack)
    landings = (k_in, v_in, vp_in, kp_in)

    def piece(ref, d, c):
        return ref.at[pl.ds(d * cap, cap), pl.ds(c * chunk_rows, chunk_rows)]

    def remote(src, dst, out_sem, in_sem, other):
        return pltpu.make_async_remote_copy(
            src_ref=src,
            dst_ref=dst,
            send_sem=out_sem,
            recv_sem=in_sem,
            device_id={"seq": other},
            device_id_type=pl.DeviceIdType.MESH,
        )

    def direct(kind, d, c, to):
        return remote(
            piece(packs[kind], d, c),
            piece(landings[kind], to, c),
            send_sem.at[kind, d, c],
            recv_sem.at[kind, to, c],
            beside[d],
        )

    def first_leg(kind, d, c):
        return remote(
            piece(packs[kind], d, c),
            relay_in.at[kind * chunks + c],
            send_sem.at[kind, d, c],
            relay_recv.at[kind, c],
            beside[d ^ 1],
        )

    def second_leg(kind, d, c):
        return remote(
            relay_in.at[kind * chunks + c],
            piece(landings[kind], d ^ 1, c),
            relay_send.at[kind, c],
            recv_sem.at[kind, d ^ 1, c],
            two_on[d],
        )

    def send(kind, d, c):
        relayed = by_relay[d][c]
        if relayed is False:

            @pl.when(inside[d])
            def _():
                direct(kind, d, c, d ^ 1).start()

        else:

            @pl.when(inside[d] & relayed)
            def _():
                first_leg(kind, d, c).start()

            @pl.when(inside[d] & jnp.logical_not(relayed))
            def _():
                direct(kind, d, c, d ^ 1).start()

    def pass_on(kind):
        for c in range(chunks):
            for d in range(nd):
                if hands_on[d][c] is not False:

                    @pl.when(hands_on[d][c])
                    def _(c=c, d=d):
                        first_leg(kind, d, c).wait_recv()
                        second_leg(kind, d, c).start()

    def arrived(kind):
        pass_on(kind)
        for d in range(nd):

            @pl.when(inside[d])
            def _(d=d):
                for c in range(chunks):
                    direct(kind, d, c, d).wait_recv()

    for kind, (full, pack) in enumerate(((k, k_pack), (v, v_pack))):
        loads[kind].wait()
        for d in range(nd):
            for s in range(cap):
                pack[d * cap + s] = full[owed_head[d][s]]
        if kind == 0:
            pl.semaphore_wait(barrier, sum(ok.astype(jnp.int32) for ok, _ in greeted))
        for c in range(chunks):
            for d in range(nd):
                send(kind, d, c)

    read_head = [table(me, beside[d], inside[d], read_slot, d) for d in range(nd)]
    blank = jnp.zeros((rows, width), q.dtype)
    k_in[none] = blank
    v_in[none] = blank
    kp_in[none] = blank
    vp_in[none] = blank
    loads[2].wait()
    loads[3].wait()

    def own_scores(h, carry):
        p32[h * E] = dot_rows(k[h], q[h]) * scale
        return carry

    lax.fori_loop(0, heads, own_scores, 0)

    arrived(0)

    def softmax(h, carry):
        scores = [p32[h * E]]
        for d in range(nd):
            slot = read_slot[d * heads + h]
            bias = jnp.where(slot == none, jnp.float32(MASKED), jnp.float32(0.0))
            scores.append(dot_rows(k_in[slot], q[h]) * scale + bias)
        top = functools.reduce(
            jnp.maximum, [jnp.max(s, axis=0, keepdims=True) for s in scores]
        )
        weights = [jnp.exp(s - top) for s in scores]
        total = sum(jnp.sum(w, axis=0, keepdims=True) for w in weights)
        inverse = 1.0 / total
        for e in range(E):
            prob = weights[e] * inverse
            p32[h * E + e] = prob
            p16[h * E + e] = prob.astype(p16.dtype)
        return carry

    lax.fori_loop(0, heads, softmax, 0)

    for d in range(nd):
        for s in range(cap):
            h = read_head[d][s]
            part = dot_plain(p16[h * E + d + 1], g[h])
            vp_pack[d * cap + s] = part.astype(vp_pack.dtype)
        for c in range(chunks):
            send(2, d, c)

    arrived(1)

    def score_grads(h, carry):
        blocks = [v[h]] + [v_in[read_slot[d * heads + h]] for d in range(nd)]
        grads = [dot_rows(block, g[h]) for block in blocks]
        delta = sum(
            jnp.sum(p32[h * E + e] * grads[e], axis=0, keepdims=True) for e in range(E)
        )
        for e in range(E):
            s16[h * E + e] = (p32[h * E + e] * (grads[e] - delta)).astype(s16.dtype)
        return carry

    lax.fori_loop(0, heads, score_grads, 0)

    for d in range(nd):
        for s in range(cap):
            h = read_head[d][s]
            part = dot_plain(s16[h * E + d + 1], q[h]) * scale
            kp_pack[d * cap + s] = part.astype(kp_pack.dtype)
        for c in range(chunks):
            send(3, d, c)

    def own_results(h, carry):
        slots = [read_slot[d * heads + h] for d in range(nd)]
        attn = dot_first(p16[h * E], v[h])
        grad = dot_first(s16[h * E], k[h])
        for d in range(nd):
            attn += dot_first(p16[h * E + d + 1], v_in[slots[d]])
            grad += dot_first(s16[h * E + d + 1], k_in[slots[d]])
        out[h] = attn.astype(out.dtype)
        qg[h] = (grad * scale).astype(qg.dtype)
        kg32[h] = dot_plain(s16[h * E], q[h]) * scale
        vg32[h] = dot_plain(p16[h * E], g[h])
        return carry

    lax.fori_loop(0, heads, own_results, 0)
    stores[0].start()
    stores[1].start()

    for kind, total, terms, result in ((0, vg32, vp_in, vg), (1, kg32, kp_in, kg)):
        arrived(2 + kind)

        def add_terms(h, carry, total=total, terms=terms, result=result):
            value = total[h]
            for d in range(nd):
                value += terms[owed_slot[d * heads + h]].astype(jnp.float32)
            result[h] = value.astype(result.dtype)
            return carry

        lax.fori_loop(0, heads, add_terms, 0)
        stores[2 + kind].start()

    for kind in range(4):
        for d in range(nd):
            for c in range(chunks):

                @pl.when(inside[d])
                def _(kind=kind, d=d, c=c):
                    direct(kind, d, c, d).wait_send()

                if hands_on[d][c] is not False:

                    @pl.when(hands_on[d][c])
                    def _(kind=kind, d=d, c=c):
                        second_leg(kind, d, c).wait_send()

    for store in stores:
        store.wait()


def write_results(*refs):
    count = (len(refs) - 2) // 3
    sources, results, held = refs[:count], refs[count : 2 * count], refs[2 * count : 3 * count]
    in_sem, out_sem = refs[3 * count :]
    loads = [pltpu.make_async_copy(a, b, in_sem.at[n]) for n, (a, b) in enumerate(zip(sources, held))]
    stores = [pltpu.make_async_copy(a, b, out_sem.at[n]) for n, (a, b) in enumerate(zip(held, results))]
    for load in loads:
        load.start()
    for load, store in zip(loads, stores):
        load.wait()
        store.start()
    for store in stores:
        store.wait()


def per_device(queries, keys, values, out_grad, tile_lists):
    heads, rows, width = queries.shape
    tile_count = lax.axis_size("seq")
    entries = tile_lists.shape[2]
    cap = HCAP * max(1, heads // 6)
    nd = len(directions(tile_count))
    E = nd + 1
    chunks = tile_count // 2 if nd == 2 else 1
    low = queries.dtype
    shape = jax.ShapeDtypeStruct(queries.shape, low)
    anywhere = pl.BlockSpec(memory_space=pl.ANY)
    whole = pltpu.VMEM(queries.shape, low)
    packed = pltpu.VMEM((nd * cap, rows, width), low)
    landed = pltpu.VMEM((nd * cap + 1, rows, width), low)
    wide = pltpu.VMEM((heads, rows, width), jnp.float32)
    results = pl.pallas_call(
        functools.partial(kernel, (tile_count, entries, cap, chunks)),
        out_shape=(shape,) * 4,
        in_specs=[pl.BlockSpec(memory_space=pltpu.SMEM)] + [anywhere] * 4,
        out_specs=(anywhere,) * 4,
        scratch_shapes=[whole] * 8
        + [
            packed,
            packed,
            landed,
            landed,
            packed,
            packed,
            landed,
            landed,
            pltpu.VMEM((heads * E, rows, rows), jnp.float32),
            pltpu.VMEM((heads * E, rows, rows), low),
            pltpu.VMEM((heads * E, rows, rows), low),
            wide,
            wide,
            pltpu.SMEM((nd * heads,), jnp.int32),
            pltpu.SMEM((nd * heads,), jnp.int32),
            pltpu.VMEM((4 * chunks, cap, rows // chunks, width), low),
            pltpu.SemaphoreType.DMA((4, nd, chunks)),
            pltpu.SemaphoreType.DMA((4, nd, chunks)),
            pltpu.SemaphoreType.DMA((4, chunks)),
            pltpu.SemaphoreType.DMA((4, chunks)),
            pltpu.SemaphoreType.DMA((4,)),
            pltpu.SemaphoreType.DMA((4,)),
        ],
        compiler_params=pltpu.CompilerParams(
            collective_id=0, has_side_effects=True, vmem_limit_bytes=60 * 1024 * 1024
        ),
        name="tile_attention",
    )(jnp.swapaxes(tile_lists, 1, 2), queries, keys, values, out_grad)
    return pl.pallas_call(
        write_results,
        out_shape=(shape,) * 4,
        in_specs=[anywhere] * 4,
        out_specs=(anywhere,) * 4,
        scratch_shapes=[whole] * 4
        + [pltpu.SemaphoreType.DMA((4,)), pltpu.SemaphoreType.DMA((4,))],
        compiler_params=pltpu.CompilerParams(vmem_limit_bytes=60 * 1024 * 1024),
        name="write_results",
    )(*results)


def solution(mesh):
    tokens = P("mp", ("clips", "seq"), None)
    return jax.shard_map(
        per_device,
        mesh=mesh,
        in_specs=(tokens, tokens, tokens, tokens, P("mp", None, None)),
        out_specs=(tokens,) * 4,
        check_vma=False,
    )
```

```python
import functools

import jax
import jax.numpy as jnp
from jax import lax
from jax.experimental import pallas as pl
from jax.experimental.pallas import tpu as pltpu
from jax.sharding import PartitionSpec as P

HCAP = 3
GX = 8
MASKED = -1e30


def directions(tile_count):
    row_tiles = min(4, tile_count // GX)
    layer_size = GX * row_tiles
    layers = tile_count // layer_size
    result = []
    for stride, extent in ((1, GX), (GX, row_tiles), (layer_size, layers)):
        if extent > 1:
            result += [(stride, extent, 1), (stride, extent, -1)]
    return result


def dot_rows(a, b):
    return lax.dot_general(a, b, (((1,), (1,)), ((), ())), preferred_element_type=jnp.float32)


def dot_plain(a, b):
    return lax.dot_general(a, b, (((1,), (0,)), ((), ())), preferred_element_type=jnp.float32)


def dot_first(a, b):
    return lax.dot_general(a, b, (((0,), (0,)), ((), ())), preferred_element_type=jnp.float32)


def kernel(
    dims,
    lists,
    q_hbm,
    k_hbm,
    v_hbm,
    g_hbm,
    out_hbm,
    qg_hbm,
    kg_hbm,
    vg_hbm,
    q,
    k,
    v,
    g,
    out,
    qg,
    kg,
    vg,
    k_pack,
    v_pack,
    k_in,
    v_in,
    kp_pack,
    vp_pack,
    kp_in,
    vp_in,
    p32,
    p16,
    s16,
    kg32,
    vg32,
    read_slot,
    owed_slot,
    relay_in,
    send_sem,
    recv_sem,
    relay_send,
    relay_recv,
    i_sem,
    o_sem,
):
    tile_count, entries, cap, chunks = dims
    heads, rows, width = q.shape
    scale = width ** (-0.5)
    dirs = directions(tile_count)
    nd = len(dirs)
    E = nd + 1
    none = nd * cap
    me = lax.axis_index("seq")

    loads = [
        pltpu.make_async_copy(src, dst, i_sem.at[n])
        for n, (src, dst) in enumerate(((k_hbm, k), (v_hbm, v), (q_hbm, q), (g_hbm, g)))
    ]
    for load in loads:
        load.start()
    stores = [
        pltpu.make_async_copy(src, dst, o_sem.at[n])
        for n, (src, dst) in enumerate(((out, out_hbm), (qg, qg_hbm), (vg, vg_hbm), (kg, kg_hbm)))
    ]

    inside, beside = [], []
    for stride, extent, sign in dirs:
        at = (me // stride) % extent + sign
        ok = (at >= 0) & (at < extent)
        inside.append(ok)
        beside.append(jnp.where(ok, me + sign * stride, me))

    chunk_rows = rows // chunks
    even, place = me % 2 == 0, me // 2
    by_relay = [[False] * chunks for _ in range(nd)]
    hands_on = [[False] * chunks for _ in range(nd)]
    two_on = []
    greeted = [(inside[d], beside[d]) for d in range(nd)]
    if chunks > 1:
        for d, (_, _, sign) in enumerate(dirs):
            amount = chunks - 1 - place if sign > 0 else place
            sends = jnp.logical_not(even) if sign > 0 else even
            by_relay[d] = [sends & (c < amount) for c in range(chunks)]
            hands_on[d] = [jnp.logical_not(sends) & (c < amount) for c in range(chunks)]
            ok = (me + 2 * sign >= 0) & (me + 2 * sign < tile_count)
            two_on.append(jnp.where(ok, me + 2 * sign, me))
            greeted.append((ok, two_on[d]))

    barrier = pltpu.get_barrier_semaphore()
    for ok, other in greeted:

        @pl.when(ok)
        def _(other=other):
            pl.semaphore_signal(
                barrier,
                inc=1,
                device_id={"seq": other},
                device_id_type=pl.DeviceIdType.MESH,
            )

    def table(reader, named, ok, slot_ref, d):
        count = jnp.int32(0)
        held = [jnp.int32(0)] * cap
        for h in range(heads):
            hit = jnp.int32(0)
            for j in range(1, entries):
                entry = lists[h, j, reader]
                hit = hit | (entry == named).astype(jnp.int32)
            hit = hit * ok.astype(jnp.int32)
            slot_ref[d * heads + h] = jnp.where(
                hit == 1, d * cap + jnp.minimum(count, cap - 1), none
            )
            held = [
                jnp.where((hit == 1) & (count == s), jnp.int32(h), held[s]) for s in range(cap)
            ]
            count = count + hit
        return held

    owed_head = [table(beside[d], me, inside[d], owed_slot, d) for d in range(nd)]
    packs = (k_pack, v_pack, vp_pack, kp_pack)
    landings = (k_in, v_in, vp_in, kp_in)

    def piece(ref, d, c):
        return ref.at[pl.ds(d * cap, cap), pl.ds(c * chunk_rows, chunk_rows)]

    def remote(src, dst, out_sem, in_sem, other):
        return pltpu.make_async_remote_copy(
            src_ref=src,
            dst_ref=dst,
            send_sem=out_sem,
            recv_sem=in_sem,
            device_id={"seq": other},
            device_id_type=pl.DeviceIdType.MESH,
        )

    def direct(kind, d, c, to):
        return remote(
            piece(packs[kind], d, c),
            piece(landings[kind], to, c),
            send_sem.at[kind, d, c],
            recv_sem.at[kind, to, c],
            beside[d],
        )

    def first_leg(kind, d, c):
        return remote(
            piece(packs[kind], d, c),
            relay_in.at[kind * chunks + c],
            send_sem.at[kind, d, c],
            relay_recv.at[kind, c],
            beside[d ^ 1],
        )

    def second_leg(kind, d, c):
        return remote(
            relay_in.at[kind * chunks + c],
            piece(landings[kind], d ^ 1, c),
            relay_send.at[kind, c],
            recv_sem.at[kind, d ^ 1, c],
            two_on[d],
        )

    def send(kind):
        for c in range(chunks):
            for d in range(nd):
                if by_relay[d][c] is not False:

                    @pl.when(inside[d] & by_relay[d][c])
                    def _(c=c, d=d):
                        first_leg(kind, d, c).start()

        for c in range(chunks):
            for d in range(nd):

                @pl.when(inside[d] & jnp.logical_not(by_relay[d][c]))
                def _(c=c, d=d):
                    direct(kind, d, c, d ^ 1).start()

    def pass_on(kind):
        for c in range(chunks):
            for d in range(nd):
                if hands_on[d][c] is not False:

                    @pl.when(hands_on[d][c])
                    def _(c=c, d=d):
                        first_leg(kind, d, c).wait_recv()
                        second_leg(kind, d, c).start()

    def arrived(kind):
        pass_on(kind)
        for d in range(nd):

            @pl.when(inside[d])
            def _(d=d):
                for c in range(chunks):
                    direct(kind, d, c, d).wait_recv()

    for kind, (full, pack) in enumerate(((k, k_pack), (v, v_pack))):
        loads[kind].wait()
        for d in range(nd):
            for s in range(cap):
                pack[d * cap + s] = full[owed_head[d][s]]
        if kind == 0:
            pl.semaphore_wait(barrier, sum(ok.astype(jnp.int32) for ok, _ in greeted))
        send(kind)

    read_head = [table(me, beside[d], inside[d], read_slot, d) for d in range(nd)]
    blank = jnp.zeros((rows, width), q.dtype)
    k_in[none] = blank
    v_in[none] = blank
    kp_in[none] = blank
    vp_in[none] = blank
    loads[2].wait()
    loads[3].wait()

    def own_scores(h, carry):
        p32[h * E] = dot_rows(k[h], q[h]) * scale
        return carry

    lax.fori_loop(0, heads, own_scores, 0)

    arrived(0)

    def softmax(h, carry):
        scores = [p32[h * E]]
        for d in range(nd):
            slot = read_slot[d * heads + h]
            bias = jnp.where(slot == none, jnp.float32(MASKED), jnp.float32(0.0))
            scores.append(dot_rows(k_in[slot], q[h]) * scale + bias)
        top = functools.reduce(
            jnp.maximum, [jnp.max(s, axis=0, keepdims=True) for s in scores]
        )
        weights = [jnp.exp(s - top) for s in scores]
        total = sum(jnp.sum(w, axis=0, keepdims=True) for w in weights)
        inverse = 1.0 / total
        for e in range(E):
            prob = weights[e] * inverse
            p32[h * E + e] = prob
            p16[h * E + e] = prob.astype(p16.dtype)
        return carry

    lax.fori_loop(0, heads, softmax, 0)

    for d in range(nd):
        for s in range(cap):
            h = read_head[d][s]
            part = dot_plain(p16[h * E + d + 1], g[h])
            vp_pack[d * cap + s] = part.astype(vp_pack.dtype)
    send(2)

    arrived(1)

    def score_grads(h, carry):
        blocks = [v[h]] + [v_in[read_slot[d * heads + h]] for d in range(nd)]
        grads = [dot_rows(block, g[h]) for block in blocks]
        delta = sum(
            jnp.sum(p32[h * E + e] * grads[e], axis=0, keepdims=True) for e in range(E)
        )
        for e in range(E):
            s16[h * E + e] = (p32[h * E + e] * (grads[e] - delta)).astype(s16.dtype)
        return carry

    lax.fori_loop(0, heads, score_grads, 0)

    for d in range(nd):
        for s in range(cap):
            h = read_head[d][s]
            part = dot_plain(s16[h * E + d + 1], q[h]) * scale
            kp_pack[d * cap + s] = part.astype(kp_pack.dtype)
    send(3)

    def own_results(h, carry):
        slots = [read_slot[d * heads + h] for d in range(nd)]
        attn = dot_first(p16[h * E], v[h])
        grad = dot_first(s16[h * E], k[h])
        for d in range(nd):
            attn += dot_first(p16[h * E + d + 1], v_in[slots[d]])
            grad += dot_first(s16[h * E + d + 1], k_in[slots[d]])
        out[h] = attn.astype(out.dtype)
        qg[h] = (grad * scale).astype(qg.dtype)
        kg32[h] = dot_plain(s16[h * E], q[h]) * scale
        vg32[h] = dot_plain(p16[h * E], g[h])
        return carry

    lax.fori_loop(0, heads, own_results, 0)
    stores[0].start()
    stores[1].start()

    for kind, total, terms, result in ((0, vg32, vp_in, vg), (1, kg32, kp_in, kg)):
        arrived(2 + kind)

        def add_terms(h, carry, total=total, terms=terms, result=result):
            value = total[h]
            for d in range(nd):
                value += terms[owed_slot[d * heads + h]].astype(jnp.float32)
            result[h] = value.astype(result.dtype)
            return carry

        lax.fori_loop(0, heads, add_terms, 0)
        stores[2 + kind].start()

    for kind in range(4):
        for d in range(nd):
            for c in range(chunks):

                @pl.when(inside[d])
                def _(kind=kind, d=d, c=c):
                    direct(kind, d, c, d).wait_send()

                if hands_on[d][c] is not False:

                    @pl.when(hands_on[d][c])
                    def _(kind=kind, d=d, c=c):
                        second_leg(kind, d, c).wait_send()

    for store in stores:
        store.wait()


def write_results(*refs):
    count = (len(refs) - 2) // 3
    sources, results, held = refs[:count], refs[count : 2 * count], refs[2 * count : 3 * count]
    in_sem, out_sem = refs[3 * count :]
    loads = [pltpu.make_async_copy(a, b, in_sem.at[n]) for n, (a, b) in enumerate(zip(sources, held))]
    stores = [pltpu.make_async_copy(a, b, out_sem.at[n]) for n, (a, b) in enumerate(zip(held, results))]
    for load in loads:
        load.start()
    for load, store in zip(loads, stores):
        load.wait()
        store.start()
    for store in stores:
        store.wait()


def per_device(queries, keys, values, out_grad, tile_lists):
    heads, rows, width = queries.shape
    tile_count = lax.axis_size("seq")
    entries = tile_lists.shape[2]
    cap = HCAP * max(1, heads // 6)
    nd = len(directions(tile_count))
    E = nd + 1
    chunks = tile_count // 2 if nd == 2 else 1
    low = queries.dtype
    shape = jax.ShapeDtypeStruct(queries.shape, low)
    anywhere = pl.BlockSpec(memory_space=pl.ANY)
    whole = pltpu.VMEM(queries.shape, low)
    packed = pltpu.VMEM((nd * cap, rows, width), low)
    landed = pltpu.VMEM((nd * cap + 1, rows, width), low)
    wide = pltpu.VMEM((heads, rows, width), jnp.float32)
    results = pl.pallas_call(
        functools.partial(kernel, (tile_count, entries, cap, chunks)),
        out_shape=(shape,) * 4,
        in_specs=[pl.BlockSpec(memory_space=pltpu.SMEM)] + [anywhere] * 4,
        out_specs=(anywhere,) * 4,
        scratch_shapes=[whole] * 8
        + [
            packed,
            packed,
            landed,
            landed,
            packed,
            packed,
            landed,
            landed,
            pltpu.VMEM((heads * E, rows, rows), jnp.float32),
            pltpu.VMEM((heads * E, rows, rows), low),
            pltpu.VMEM((heads * E, rows, rows), low),
            wide,
            wide,
            pltpu.SMEM((nd * heads,), jnp.int32),
            pltpu.SMEM((nd * heads,), jnp.int32),
            pltpu.VMEM((4 * chunks, cap, rows // chunks, width), low),
            pltpu.SemaphoreType.DMA((4, nd, chunks)),
            pltpu.SemaphoreType.DMA((4, nd, chunks)),
            pltpu.SemaphoreType.DMA((4, chunks)),
            pltpu.SemaphoreType.DMA((4, chunks)),
            pltpu.SemaphoreType.DMA((4,)),
            pltpu.SemaphoreType.DMA((4,)),
        ],
        compiler_params=pltpu.CompilerParams(
            collective_id=0, has_side_effects=True, vmem_limit_bytes=60 * 1024 * 1024
        ),
        name="tile_attention",
    )(jnp.swapaxes(tile_lists, 1, 2), queries, keys, values, out_grad)
    return pl.pallas_call(
        write_results,
        out_shape=(shape,) * 4,
        in_specs=[anywhere] * 4,
        out_specs=(anywhere,) * 4,
        scratch_shapes=[whole] * 4
        + [pltpu.SemaphoreType.DMA((4,)), pltpu.SemaphoreType.DMA((4,))],
        compiler_params=pltpu.CompilerParams(vmem_limit_bytes=60 * 1024 * 1024),
        name="write_results",
    )(*results)


def solution(mesh):
    tokens = P("mp", ("clips", "seq"), None)
    return jax.shard_map(
        per_device,
        mesh=mesh,
        in_specs=(tokens, tokens, tokens, tokens, P("mp", None, None)),
        out_specs=(tokens,) * 4,
        check_vma=False,
    )
```
